32 devices in a mesh: patch: 4 (over y, x), uly: 8 (over z, core).
Axes of the slice: x: 2, y: 2, z: 4, core: 2. Of those that a mesh axis runs over, the one named last changes fastest.
Arguments:
- queries: bfloat16 [512, 3072], P(('patch', 'uly')), may hold values from -512 to 512
- keys_new: bfloat16 [512, 3072], P(('patch', 'uly')), may hold values from -6 to 6
- values_new: bfloat16 [512, 3072], P(('patch', 'uly')), may hold values from -6 to 6
- keys_old: bfloat16 [512, 3072], P(('patch', 'uly')), may hold values from -8 to 8
- values_old: bfloat16 [512, 3072], P(('patch', 'uly')), may hold values from -6 to 6
- gate_table: float32 [50, 3072], replicated, may hold values from 0.5 to 2
- step_index: int32 [1], replicated, may hold values from 0 to 49
Outputs:
- attended: bfloat16 [512, 3072], P(('patch', 'uly'))
The draws below stay inside these ranges and needn't reach their ends.
All inputs are finite; a program needn't handle non-finite values.
Results may differ from the reference program's by a relative error of at most 0.0045.
Values may be sent and summed in bfloat16 or wider, within the bound.
No kernel may reach another device: no remote copies, remote signals or barrier semaphores. Data moves between devices by JAX's collectives and lax.ppermute only.
A program may use at most 64 MiB of HBM per device.

```python
import math
import jax
import jax.numpy as jnp
from jax import lax

HEADS = 24
HEAD_DIM = 128
TOK_DEV = 16
STEPS = 50
D = 3072
TOKENS = 512
N_PATCH = 4
N_ULY = 8


def shared_fields(key):
    query_key = jax.random.fold_in(key, 11)
    stale_key = jax.random.fold_in(key, 23)
    query_field = jnp.clip(3.0 * jax.random.normal(query_key, (TOKENS, D), jnp.float32), -18.0, 18.0)
    stale_field = jnp.clip(jax.random.normal(stale_key, (TOKENS, D), jnp.float32), -6.0, 6.0)
    return (query_field, stale_field)


def draw_queries(key, part):
    return shared_fields(key)[0].astype(jnp.bfloat16)


def draw_keys_old(key, part):
    return shared_fields(key)[1].astype(jnp.bfloat16)


def levels(key, extent, shards, smallest, high):
    factor_of, own = 1.0, jax.random.fold_in(key, 6)
    for axis_at, blocks in shards:
        steps = jnp.exp(jax.random.uniform(jax.random.fold_in(own, axis_at), (blocks,), jnp.float32, smallest / len(shards), high / len(shards)))
        factor_of = factor_of * jnp.repeat(steps, extent[axis_at] // blocks).reshape([-1 if axis == axis_at else 1 for axis in range(len(extent))])
    return factor_of


def scatter_about(key, extent, deviation, bound, split=(), held_as=jnp.bfloat16):
    entries = jax.random.normal(key, extent, jnp.float32) * deviation
    if len(split) > 0:
        entries = levels(key, extent, split, -0.22, 0.18) * entries
    return jnp.clip(entries, min=-bound, max=bound).astype(held_as)


def setup_inputs(seed: int = 0) -> dict:
    streams_of = jax.random.split(jax.random.key(seed), 8)
    queries = draw_queries(jax.random.fold_in(streams_of[7], 71), 0)
    keys_new = scatter_about(streams_of[1], (TOKENS, D), 1.0, 6.0, ((0, 32),))
    values_new = scatter_about(streams_of[2], (TOKENS, D), 1.0, 6.0, ((0, 32),))
    keys_old = draw_keys_old(jax.random.fold_in(streams_of[7], 71), 0)
    values_old = scatter_about(streams_of[4], (TOKENS, D), 1.0, 6.0, ((0, 32),))
    gate_table = jnp.clip(jnp.exp(jax.random.uniform(streams_of[5], (STEPS, D), jnp.float32, math.log(0.5), math.log(2.0))), 0.5, 2.0)
    step_index = jax.random.randint(streams_of[6], (1,), 0, STEPS).astype(jnp.int32)
    return dict(queries=queries, keys_new=keys_new, values_new=values_new, keys_old=keys_old, values_old=values_old, gate_table=gate_table, step_index=step_index)


def reference(queries, keys_new, values_new, keys_old, values_old, gate_table, step_index):
    rows = TOK_DEV * N_ULY
    total_rows = rows * N_PATCH
    scale = HEAD_DIM ** -0.5
    picker = (jnp.arange(STEPS, dtype=jnp.int32) == step_index[0]).astype(jnp.float32)
    gate = jnp.dot(picker, gate_table, precision=lax.Precision.HIGHEST)
    old_keys = keys_old.astype(jnp.float32).reshape(total_rows, HEADS, HEAD_DIM)
    old_values = values_old.astype(jnp.float32).reshape(total_rows, HEADS, HEAD_DIM)
    positions = jnp.arange(total_rows, dtype=jnp.int32)

    def one_patch(patch_id):
        start = (patch_id * rows).astype(jnp.int32)
        query_block = lax.dynamic_slice_in_dim(queries, start, rows, 0).astype(jnp.float32).reshape(rows, HEADS, HEAD_DIM)
        key_block = lax.dynamic_slice_in_dim(keys_new, start, rows, 0).astype(jnp.float32).reshape(rows, HEADS, HEAD_DIM)
        value_block = lax.dynamic_slice_in_dim(values_new, start, rows, 0).astype(jnp.float32).reshape(rows, HEADS, HEAD_DIM)
        score_old = jnp.einsum("phd,khd->hpk", query_block, old_keys) * scale
        score_new = jnp.einsum("phd,khd->hpk", query_block, key_block) * scale
        own = (positions // rows) == patch_id
        score_old = jnp.where(own[None, None, :], jnp.float32(-1e30), score_old)
        rowmax = jnp.maximum(jnp.max(score_old, axis=-1), jnp.max(score_new, axis=-1))
        expo_old = jnp.exp(score_old - rowmax[..., None])
        expo_new = jnp.exp(score_new - rowmax[..., None])
        total = jnp.sum(expo_old, axis=-1) + jnp.sum(expo_new, axis=-1)
        weight_old = lax.optimization_barrier(expo_old.astype(jnp.bfloat16)).astype(jnp.float32)
        weight_new = lax.optimization_barrier(expo_new.astype(jnp.bfloat16)).astype(jnp.float32)
        summed = jnp.einsum("hpk,khd->phd", weight_old, old_values) + jnp.einsum("hpk,khd->phd", weight_new, value_block)
        mixed = summed / jnp.transpose(total)[..., None]
        return (mixed.reshape(rows, HEADS * HEAD_DIM) * gate).astype(jnp.bfloat16)

    blocks = lax.map(one_patch, jnp.arange(N_PATCH, dtype=jnp.int32))
    return blocks.reshape(total_rows, HEADS * HEAD_DIM)
```

```python
import functools

import jax
import jax.numpy as jnp
from jax import lax
from jax.experimental import pallas as pl
from jax.experimental.pallas import tpu as pltpu
from jax.sharding import PartitionSpec as P

HEADS = 24
HEAD_DIM = 128
MAX_DIRECT = 8


def absorb(carry, query_heads, key_piece, value_piece, masked):
    run_max, run_total, accumulated = carry
    score = jnp.einsum(
        "phd,khd->hpk", query_heads, key_piece, preferred_element_type=jnp.float32
    ) * HEAD_DIM ** (-0.5)
    score = jnp.where(masked[None, None, :], jnp.float32(-1e30), score)
    new_max = jnp.maximum(run_max, jnp.max(score, axis=-1))
    shrink = jnp.exp(run_max - new_max)
    expo = jnp.exp(score - new_max[..., None])
    run_total = run_total * shrink + jnp.sum(expo, axis=-1)
    update = jnp.einsum(
        "hpk,khd->phd", expo.astype(jnp.bfloat16), value_piece, preferred_element_type=jnp.float32
    )
    accumulated = accumulated * jnp.transpose(shrink)[..., None] + update
    return (new_max, run_total, accumulated)


def absorb_blocks(carry, query_heads, key_piece, value_piece, masked):
    count = key_piece.shape[0]
    span = 2048
    if count > span and count % span == 0:
        heads_here = key_piece.shape[1]
        key_blocks = key_piece.reshape(count // span, span, heads_here, HEAD_DIM)
        value_blocks = value_piece.reshape(count // span, span, heads_here, HEAD_DIM)
        mask_blocks = masked.reshape(count // span, span)

        def one_block(state, pieces):
            return (absorb(state, query_heads, pieces[0], pieces[1], pieces[2]), None)

        carry, unused = lax.scan(one_block, carry, (key_blocks, value_blocks, mask_blocks))
        return carry
    return absorb(carry, query_heads, key_piece, value_piece, masked)


def body_many(queries, keys_new, values_new, keys_old, values_old, gate_table, step_index):
    groups = lax.axis_size("uly")
    heads_here = HEADS // groups
    width_here = heads_here * HEAD_DIM
    patch_here = lax.axis_index("patch")
    fresh = (
        lax.all_to_all(queries, "uly", split_axis=1, concat_axis=0, tiled=True),
        lax.all_to_all(keys_new, "uly", split_axis=1, concat_axis=0, tiled=True),
        lax.all_to_all(values_new, "uly", split_axis=1, concat_axis=0, tiled=True),
    )
    query_heads = fresh[0].reshape(-1, heads_here, HEAD_DIM)
    fresh_keys = fresh[1].reshape(-1, heads_here, HEAD_DIM)
    fresh_values = fresh[2].reshape(-1, heads_here, HEAD_DIM)
    patch_rows = query_heads.shape[0]
    score = jnp.einsum(
        "phd,khd->hpk", query_heads, fresh_keys, preferred_element_type=jnp.float32
    ) * HEAD_DIM ** (-0.5)
    run_max = jnp.max(score, axis=-1)
    expo = jnp.exp(score - run_max[..., None])
    run_total = jnp.sum(expo, axis=-1)
    accumulated = jnp.einsum(
        "hpk,khd->phd", expo.astype(jnp.bfloat16), fresh_values, preferred_element_type=jnp.float32
    )
    carry = (run_max, run_total, accumulated)
    stale = (
        lax.all_to_all(keys_old, "uly", split_axis=1, concat_axis=0, tiled=True),
        lax.all_to_all(values_old, "uly", split_axis=1, concat_axis=0, tiled=True),
    )
    stale_keys = stale[0].reshape(-1, heads_here, HEAD_DIM)
    stale_values = stale[1].reshape(-1, heads_here, HEAD_DIM)
    pieces = (
        lax.all_gather(stale_keys, "patch", axis=0, tiled=True),
        lax.all_gather(stale_values, "patch", axis=0, tiled=True),
    )
    count = pieces[0].shape[0]
    masked = jnp.arange(count, dtype=jnp.int32) // patch_rows == patch_here
    carry = absorb_blocks(carry, query_heads, pieces[0], pieces[1], masked)
    run_max, run_total, accumulated = carry
    picker = (jnp.arange(gate_table.shape[0], dtype=jnp.int32) == step_index[0]).astype(jnp.float32)
    gate = jnp.dot(picker, gate_table, precision=lax.Precision.HIGHEST)
    gate_here = lax.dynamic_slice_in_dim(gate, lax.axis_index("uly") * width_here, width_here, 0)
    mixed = (accumulated / jnp.transpose(run_total)[..., None]).reshape(patch_rows, width_here)
    gated = (mixed * gate_here).astype(jnp.bfloat16)
    return lax.all_to_all(gated, "uly", split_axis=0, concat_axis=1, tiled=True)


def partner(here, step, count):
    if count & (count - 1) == 0:
        return here ^ step
    return (here + step) % count


def source(here, step, count):
    if count & (count - 1) == 0:
        return here ^ step
    return (here - step) % count


def far_first(count):
    order = []
    for low in reversed(range(0, count, 2)):
        order += [step for step in (low, low + 1) if 0 < step < count]
    return order


def shift(array, axis, step, count):
    return lax.ppermute(array, axis, [(i, partner(i, step, count)) for i in range(count)])


def pack_kernel(steps, groups, width, index_ref, *refs):
    count = len(refs) - len(steps)
    here = index_ref[0]
    for step, out_ref in zip(steps, refs[count:], strict=True):
        column = pl.multiple_of(partner(here, step, groups) * width, HEAD_DIM)
        for place, ref in enumerate(refs[:count]):
            rows = ref.shape[0]
            out_ref[pl.ds(place * rows, rows), :] = ref[:, pl.ds(column, width)]


def pack(index, arrays, steps, groups, width, name):
    rows = arrays[0].shape[0] * len(arrays)
    piece = jax.ShapeDtypeStruct((rows, width), arrays[0].dtype)
    vmem = pl.BlockSpec(memory_space=pltpu.VMEM)
    return pl.pallas_call(
        functools.partial(pack_kernel, steps, groups, width),
        out_shape=[piece] * len(steps),
        in_specs=[pl.BlockSpec(memory_space=pltpu.SMEM)] + [vmem] * len(arrays),
        out_specs=[vmem] * len(steps),
        name=name,
    )(index, *arrays)


def attend_kernel(steps, groups, rows, heads_here, others, index_ref, gate_ref, *refs):
    fresh = refs[:groups]
    stale = refs[groups : groups + others]
    outs = refs[groups + others : groups + others + groups]
    mixed_ref = refs[-1]
    here = index_ref[0]
    nearest = (((1,), (1,)), ((), ()))
    plain = (((1,), (0,)), ((), ()))
    for head in range(heads_here):
        columns = slice(head * HEAD_DIM, (head + 1) * HEAD_DIM)
        query = jnp.concatenate([r[0:rows, columns] for r in fresh], axis=0)
        keys = [r[rows : 2 * rows, columns] for r in fresh]
        values = [r[2 * rows : 3 * rows, columns] for r in fresh]
        for r in stale:
            keys += [r[i, 0:rows, columns] for i in range(groups)]
            values += [r[i, rows : 2 * rows, columns] for i in range(groups)]
        key = jnp.concatenate(keys, axis=0)
        value = jnp.concatenate(values, axis=0)
        score = lax.dot_general(
            query, key, nearest, preferred_element_type=jnp.float32
        ) * HEAD_DIM ** (-0.5)
        expo = jnp.exp(score - jnp.max(score, axis=-1, keepdims=True))
        total = jnp.sum(expo, axis=-1, keepdims=True)
        summed = lax.dot_general(
            expo.astype(jnp.bfloat16), value, plain, preferred_element_type=jnp.float32
        )
        gated = (summed / total) * gate_ref[0:1, columns]
        gated = gated.astype(jnp.bfloat16)
        for place in range(groups):
            owner = source(here, steps[place], groups)
            start = pl.multiple_of(owner * rows, rows)
            mixed_ref[pl.ds(start, rows), columns] = gated[place * rows : (place + 1) * rows, :]
    for place in range(groups):
        start = pl.multiple_of(partner(here, steps[place], groups) * rows, rows)
        outs[place][...] = mixed_ref[pl.ds(start, rows), :]


def join_kernel(steps, groups, width, index_ref, *refs):
    out_ref = refs[-1]
    here = index_ref[0]
    for step, ref in zip(steps, refs[:-1], strict=True):
        column = pl.multiple_of(source(here, step, groups) * width, HEAD_DIM)
        out_ref[:, pl.ds(column, width)] = ref[...]


def body_few(queries, keys_new, values_new, keys_old, values_old, gate_table, step_index):
    groups = lax.axis_size("uly")
    patches = lax.axis_size("patch")
    heads_here = HEADS // groups
    width = heads_here * HEAD_DIM
    rows = queries.shape[0]
    here = lax.axis_index("uly")
    index = here.astype(jnp.int32).reshape(1)
    steps = [0] + far_first(groups)
    vmem = pl.BlockSpec(memory_space=pltpu.VMEM)
    smem = pl.BlockSpec(memory_space=pltpu.SMEM)

    def exchange(pieces):
        return [pieces[0]] + [
            shift(piece, "uly", step, groups)
            for step, piece in zip(steps[1:], pieces[1:], strict=True)
        ]

    stale_pieces = exchange(pack(index, (keys_old, values_old), steps, groups, width, "pack_stale"))
    fresh_out = pack(index, (queries, keys_new, values_new), steps, groups, width, "pack_fresh")
    stale_here = jnp.stack(stale_pieces)
    stale_here, fresh_out = lax.optimization_barrier((stale_here, fresh_out))
    stale = [shift(stale_here, "patch", step, patches) for step in reversed(range(1, patches))]
    fresh = exchange(fresh_out)
    gate_here = lax.dynamic_slice(gate_table, (step_index[0], here * width), (1, width))

    piece = jax.ShapeDtypeStruct((rows, width), jnp.bfloat16)
    attended = pl.pallas_call(
        functools.partial(attend_kernel, steps, groups, rows, heads_here, len(stale)),
        out_shape=[piece] * groups,
        in_specs=[smem, vmem] + [vmem] * (groups + len(stale)),
        out_specs=[vmem] * groups,
        scratch_shapes=[pltpu.VMEM((groups * rows, width), jnp.bfloat16)],
        name="attend",
    )(index, gate_here, *fresh, *stale)
    pieces = exchange(attended)
    return pl.pallas_call(
        functools.partial(join_kernel, steps, groups, width),
        out_shape=jax.ShapeDtypeStruct((rows, groups * width), jnp.bfloat16),
        in_specs=[smem] + [vmem] * groups,
        out_specs=vmem,
        name="join",
    )(index, *pieces)


def solution(mesh):
    body = body_few if mesh.shape["patch"] <= MAX_DIRECT else body_many
    in_specs = (
        P(("patch", "uly"), None),
        P(("patch", "uly"), None),
        P(("patch", "uly"), None),
        P(("patch", "uly"), None),
        P(("patch", "uly"), None),
        P(),
        P(),
    )
    out_specs = P(("patch", "uly"), None)
    return jax.shard_map(body, mesh=mesh, in_specs=in_specs, out_specs=out_specs, check_vma=False)
```

```python
import functools

import jax
import jax.numpy as jnp
from jax import lax
from jax.experimental import pallas as pl
from jax.experimental.pallas import tpu as pltpu
from jax.sharding import PartitionSpec as P

HEADS = 24
HEAD_DIM = 128
MAX_DIRECT = 8


def absorb(carry, query_heads, key_piece, value_piece, masked):
    run_max, run_total, accumulated = carry
    score = jnp.einsum(
        "phd,khd->hpk", query_heads, key_piece, preferred_element_type=jnp.float32
    ) * HEAD_DIM ** (-0.5)
    score = jnp.where(masked[None, None, :], jnp.float32(-1e30), score)
    new_max = jnp.maximum(run_max, jnp.max(score, axis=-1))
    shrink = jnp.exp(run_max - new_max)
    expo = jnp.exp(score - new_max[..., None])
    run_total = run_total * shrink + jnp.sum(expo, axis=-1)
    update = jnp.einsum(
        "hpk,khd->phd", expo.astype(jnp.bfloat16), value_piece, preferred_element_type=jnp.float32
    )
    accumulated = accumulated * jnp.transpose(shrink)[..., None] + update
    return (new_max, run_total, accumulated)


def absorb_blocks(carry, query_heads, key_piece, value_piece, masked):
    count = key_piece.shape[0]
    span = 2048
    if count > span and count % span == 0:
        heads_here = key_piece.shape[1]
        key_blocks = key_piece.reshape(count // span, span, heads_here, HEAD_DIM)
        value_blocks = value_piece.reshape(count // span, span, heads_here, HEAD_DIM)
        mask_blocks = masked.reshape(count // span, span)

        def one_block(state, pieces):
            return (absorb(state, query_heads, pieces[0], pieces[1], pieces[2]), None)

        carry, unused = lax.scan(one_block, carry, (key_blocks, value_blocks, mask_blocks))
        return carry
    return absorb(carry, query_heads, key_piece, value_piece, masked)


def body_many(queries, keys_new, values_new, keys_old, values_old, gate_table, step_index):
    groups = lax.axis_size("uly")
    heads_here = HEADS // groups
    width_here = heads_here * HEAD_DIM
    patch_here = lax.axis_index("patch")
    fresh = (
        lax.all_to_all(queries, "uly", split_axis=1, concat_axis=0, tiled=True),
        lax.all_to_all(keys_new, "uly", split_axis=1, concat_axis=0, tiled=True),
        lax.all_to_all(values_new, "uly", split_axis=1, concat_axis=0, tiled=True),
    )
    query_heads = fresh[0].reshape(-1, heads_here, HEAD_DIM)
    fresh_keys = fresh[1].reshape(-1, heads_here, HEAD_DIM)
    fresh_values = fresh[2].reshape(-1, heads_here, HEAD_DIM)
    patch_rows = query_heads.shape[0]
    score = jnp.einsum(
        "phd,khd->hpk", query_heads, fresh_keys, preferred_element_type=jnp.float32
    ) * HEAD_DIM ** (-0.5)
    run_max = jnp.max(score, axis=-1)
    expo = jnp.exp(score - run_max[..., None])
    run_total = jnp.sum(expo, axis=-1)
    accumulated = jnp.einsum(
        "hpk,khd->phd", expo.astype(jnp.bfloat16), fresh_values, preferred_element_type=jnp.float32
    )
    carry = (run_max, run_total, accumulated)
    stale = (
        lax.all_to_all(keys_old, "uly", split_axis=1, concat_axis=0, tiled=True),
        lax.all_to_all(values_old, "uly", split_axis=1, concat_axis=0, tiled=True),
    )
    stale_keys = stale[0].reshape(-1, heads_here, HEAD_DIM)
    stale_values = stale[1].reshape(-1, heads_here, HEAD_DIM)
    pieces = (
        lax.all_gather(stale_keys, "patch", axis=0, tiled=True),
        lax.all_gather(stale_values, "patch", axis=0, tiled=True),
    )
    count = pieces[0].shape[0]
    masked = jnp.arange(count, dtype=jnp.int32) // patch_rows == patch_here
    carry = absorb_blocks(carry, query_heads, pieces[0], pieces[1], masked)
    run_max, run_total, accumulated = carry
    picker = (jnp.arange(gate_table.shape[0], dtype=jnp.int32) == step_index[0]).astype(jnp.float32)
    gate = jnp.dot(picker, gate_table, precision=lax.Precision.HIGHEST)
    gate_here = lax.dynamic_slice_in_dim(gate, lax.axis_index("uly") * width_here, width_here, 0)
    mixed = (accumulated / jnp.transpose(run_total)[..., None]).reshape(patch_rows, width_here)
    gated = (mixed * gate_here).astype(jnp.bfloat16)
    return lax.all_to_all(gated, "uly", split_axis=0, concat_axis=1, tiled=True)


def steps_of(count):
    return [0] + list(reversed(range(1, count)))


def partner(here, step, count):
    if count & (count - 1) == 0:
        return here ^ step
    return (here + step) % count


def source(here, step, count):
    if count & (count - 1) == 0:
        return here ^ step
    return (here - step) % count


def shift(array, axis, step, lane, count, way=partner):
    pairs = [(i * lane + j, way(i, step, count) * lane + j) for i in range(count) for j in range(lane)]
    return lax.ppermute(array, axis, pairs)


def swap(array):
    return lax.ppermute(array, "uly", [(i, i ^ 1) for i in range(lax.axis_size("uly"))])


def in_vmem(array):
    return pltpu.with_memory_space_constraint(array, pltpu.VMEM)


def pack_kernel(steps, levels, lane, width, index_ref, *refs):
    count = len(refs) - len(steps)
    level = index_ref[0] // lane
    offset = index_ref[0] % lane
    for step, out_ref in zip(steps, refs[count:], strict=True):
        owner = partner(level, step, levels) * lane + offset
        column = pl.multiple_of(owner * width, HEAD_DIM)
        for place, ref in enumerate(refs[:count]):
            rows = ref.shape[0]
            out_ref[pl.ds(place * rows, rows), :] = ref[:, pl.ds(column, width)]


def pack(index, arrays, steps, levels, lane, width, name):
    rows = arrays[0].shape[0] * len(arrays)
    vmem = pl.BlockSpec(memory_space=pltpu.VMEM)
    return pl.pallas_call(
        functools.partial(pack_kernel, steps, levels, lane, width),
        out_shape=[pltpu.VMEM((rows, width), arrays[0].dtype)] * len(steps),
        in_specs=[pl.BlockSpec(memory_space=pltpu.SMEM)] + [vmem] * len(arrays),
        out_specs=[vmem] * len(steps),
        name=name,
    )(index, *arrays)


def attend_kernel(levels, rows, heads_here, others, gate_ref, *refs):
    fresh = refs[:levels]
    stale = refs[levels : levels + others]
    outs = refs[levels + others :]
    nearest = (((1,), (1,)), ((), ()))
    plain = (((1,), (0,)), ((), ()))
    for head in range(heads_here):
        columns = slice(head * HEAD_DIM, (head + 1) * HEAD_DIM)
        query = jnp.concatenate([r[0:rows, columns] for r in fresh], axis=0)
        keys = [r[rows : 2 * rows, columns] for r in fresh]
        values = [r[2 * rows : 3 * rows, columns] for r in fresh]
        for r in stale:
            keys += [r[i, 0:rows, columns] for i in range(levels)]
            values += [r[i, rows : 2 * rows, columns] for i in range(levels)]
        key = jnp.concatenate(keys, axis=0)
        value = jnp.concatenate(values, axis=0)
        score = lax.dot_general(
            query, key, nearest, preferred_element_type=jnp.float32
        ) * HEAD_DIM ** (-0.5)
        expo = jnp.exp(score - jnp.max(score, axis=-1, keepdims=True))
        total = jnp.sum(expo, axis=-1, keepdims=True)
        summed = lax.dot_general(
            expo.astype(jnp.bfloat16), value, plain, preferred_element_type=jnp.float32
        )
        gated = ((summed / total) * gate_ref[0:1, columns]).astype(jnp.bfloat16)
        for place in range(levels):
            outs[place][:, columns] = gated[place * rows : (place + 1) * rows, :]


def join_kernel(steps, levels, lane, rows, width, index_ref, swapped_ref, *refs):
    out_ref = refs[-1]
    level = index_ref[0] // lane
    offset = index_ref[0] % lane
    for place, (step, ref) in enumerate(zip(steps, refs[:-1], strict=True)):
        owner = source(level, step, levels) * lane
        column = pl.multiple_of((owner + offset) * width, HEAD_DIM)
        out_ref[:, pl.ds(column, width)] = ref[0:rows, :]
        column = pl.multiple_of((owner + 1 - offset) * width, HEAD_DIM)
        out_ref[:, pl.ds(column, width)] = swapped_ref[place]


def body_few(queries, keys_new, values_new, keys_old, values_old, gate_table, step_index):
    groups = lax.axis_size("uly")
    patches = lax.axis_size("patch")
    lane = 2
    levels = groups // lane
    width = HEADS // groups * HEAD_DIM
    rows = queries.shape[0]
    here = lax.axis_index("uly")
    index = here.astype(jnp.int32).reshape(1)
    steps = steps_of(levels)
    vmem = pl.BlockSpec(memory_space=pltpu.VMEM)
    smem = pl.BlockSpec(memory_space=pltpu.SMEM)

    def exchange(pieces, way):
        return [pieces[0]] + [
            shift(piece, "uly", step, lane, levels, way)
            for step, piece in zip(steps[1:], pieces[1:], strict=True)
        ]

    def spread(arrays, name):
        both = [side for array in arrays for side in (array, in_vmem(swap(array)))]
        return pack(index, both, steps, levels, lane, width, name)

    stale_here = jnp.stack(exchange(spread((keys_old, values_old), "pack_stale"), partner))
    fresh_out = spread((queries, keys_new, values_new), "pack_fresh")
    gate_here = lax.dynamic_slice(gate_table, (step_index[0], here * width), (1, width))
    stale_here, fresh_out, gate_here = lax.optimization_barrier((stale_here, fresh_out, gate_here))
    stale = [shift(stale_here, "patch", step, 1, patches) for step in reversed(range(1, patches))]
    fresh = exchange(fresh_out, partner)

    attended = pl.pallas_call(
        functools.partial(attend_kernel, levels, lane * rows, HEADS // groups, len(stale)),
        out_shape=[pltpu.VMEM((lane * rows, width), jnp.bfloat16)] * levels,
        in_specs=[vmem] * (1 + levels + len(stale)),
        out_specs=[vmem] * levels,
        name="attend",
    )(*[in_vmem(x) for x in (gate_here, *fresh, *stale)])
    pieces = exchange(attended, source)
    swapped = swap(jnp.stack([piece[rows:] for piece in pieces]))
    return pl.pallas_call(
        functools.partial(join_kernel, steps, levels, lane, rows, width),
        out_shape=jax.ShapeDtypeStruct((rows, groups * width), jnp.bfloat16),
        in_specs=[smem] + [vmem] * (1 + levels),
        out_specs=vmem,
        name="join",
    )(index, *[in_vmem(x) for x in (swapped, *pieces)])


def solution(mesh):
    direct = mesh.shape["patch"] <= MAX_DIRECT and mesh.shape["uly"] % 2 == 0
    body = body_few if direct else body_many
    in_specs = (
        P(("patch", "uly"), None),
        P(("patch", "uly"), None),
        P(("patch", "uly"), None),
        P(("patch", "uly"), None),
        P(("patch", "uly"), None),
        P(),
        P(),
    )
    out_specs = P(("patch", "uly"), None)
    return jax.shard_map(body, mesh=mesh, in_specs=in_specs, out_specs=out_specs, check_vma=False)
```

```python
import functools

import jax
import jax.numpy as jnp
from jax import lax
from jax.experimental import pallas as pl
from jax.experimental.pallas import tpu as pltpu
from jax.sharding import PartitionSpec as P


HEADS = 24
HEAD_DIM = 128
MAX_DIRECT = 8


def absorb(carry, query_heads, key_piece, value_piece, masked):
    run_max, run_total, accumulated = carry
    score = jnp.einsum(
        "phd,khd->hpk", query_heads, key_piece, preferred_element_type=jnp.float32
    ) * HEAD_DIM ** (-0.5)
    score = jnp.where(masked[None, None, :], jnp.float32(-1e30), score)
    new_max = jnp.maximum(run_max, jnp.max(score, axis=-1))
    shrink = jnp.exp(run_max - new_max)
    expo = jnp.exp(score - new_max[..., None])
    run_total = run_total * shrink + jnp.sum(expo, axis=-1)
    update = jnp.einsum(
        "hpk,khd->phd", expo.astype(jnp.bfloat16), value_piece, preferred_element_type=jnp.float32
    )
    accumulated = accumulated * jnp.transpose(shrink)[..., None] + update
    return (new_max, run_total, accumulated)


def absorb_blocks(carry, query_heads, key_piece, value_piece, masked):
    count = key_piece.shape[0]
    span = 2048
    if count > span and count % span == 0:
        heads_here = key_piece.shape[1]
        key_blocks = key_piece.reshape(count // span, span, heads_here, HEAD_DIM)
        value_blocks = value_piece.reshape(count // span, span, heads_here, HEAD_DIM)
        mask_blocks = masked.reshape(count // span, span)

        def one_block(state, pieces):
            return (absorb(state, query_heads, pieces[0], pieces[1], pieces[2]), None)

        carry, _ = lax.scan(one_block, carry, (key_blocks, value_blocks, mask_blocks))
        return carry
    return absorb(carry, query_heads, key_piece, value_piece, masked)


def body_many(queries, keys_new, values_new, keys_old, values_old, gate_table, step_index):
    groups = lax.axis_size("uly")
    heads_here = HEADS // groups
    width_here = heads_here * HEAD_DIM
    patch_here = lax.axis_index("patch")
    fresh = (
        lax.all_to_all(queries, "uly", split_axis=1, concat_axis=0, tiled=True),
        lax.all_to_all(keys_new, "uly", split_axis=1, concat_axis=0, tiled=True),
        lax.all_to_all(values_new, "uly", split_axis=1, concat_axis=0, tiled=True),
    )
    query_heads = fresh[0].reshape(-1, heads_here, HEAD_DIM)
    fresh_keys = fresh[1].reshape(-1, heads_here, HEAD_DIM)
    fresh_values = fresh[2].reshape(-1, heads_here, HEAD_DIM)
    patch_rows = query_heads.shape[0]
    score = jnp.einsum(
        "phd,khd->hpk", query_heads, fresh_keys, preferred_element_type=jnp.float32
    ) * HEAD_DIM ** (-0.5)
    run_max = jnp.max(score, axis=-1)
    expo = jnp.exp(score - run_max[..., None])
    run_total = jnp.sum(expo, axis=-1)
    accumulated = jnp.einsum(
        "hpk,khd->phd", expo.astype(jnp.bfloat16), fresh_values, preferred_element_type=jnp.float32
    )
    carry = (run_max, run_total, accumulated)
    stale = (
        lax.all_to_all(keys_old, "uly", split_axis=1, concat_axis=0, tiled=True),
        lax.all_to_all(values_old, "uly", split_axis=1, concat_axis=0, tiled=True),
    )
    stale_keys = stale[0].reshape(-1, heads_here, HEAD_DIM)
    stale_values = stale[1].reshape(-1, heads_here, HEAD_DIM)
    pieces = (
        lax.all_gather(stale_keys, "patch", axis=0, tiled=True),
        lax.all_gather(stale_values, "patch", axis=0, tiled=True),
    )
    count = pieces[0].shape[0]
    masked = jnp.arange(count, dtype=jnp.int32) // patch_rows == patch_here
    carry = absorb_blocks(carry, query_heads, pieces[0], pieces[1], masked)
    run_max, run_total, accumulated = carry
    picker = (jnp.arange(gate_table.shape[0], dtype=jnp.int32) == step_index[0]).astype(jnp.float32)
    gate = jnp.dot(picker, gate_table, precision=lax.Precision.HIGHEST)
    gate_here = lax.dynamic_slice_in_dim(gate, lax.axis_index("uly") * width_here, width_here, 0)
    mixed = (accumulated / jnp.transpose(run_total)[..., None]).reshape(patch_rows, width_here)
    gated = (mixed * gate_here).astype(jnp.bfloat16)
    return lax.all_to_all(gated, "uly", split_axis=0, concat_axis=1, tiled=True)


def steps_of(count):
    return [0] + list(range(max(count // 2, 1), count)) + list(reversed(range(1, count // 2)))


def out_steps_of(count):
    return [0] + [step for step in (count - 1, *range(1, count - 1)) if step > 0]


def partner(here, step, count):
    if count & (count - 1) == 0:
        return here ^ step
    return (here + step) % count


def source(here, step, count):
    if count & (count - 1) == 0:
        return here ^ step
    return (here - step) % count


def shift(array, axis, step, lane, count, way=partner):
    pairs = [(i * lane + j, way(i, step, count) * lane + j) for i in range(count) for j in range(lane)]
    return lax.ppermute(array, axis, pairs)


def swap(array):
    return lax.ppermute(array, "uly", [(i, i ^ 1) for i in range(lax.axis_size("uly"))])


def in_vmem(array):
    return pltpu.with_memory_space_constraint(array, pltpu.VMEM)


def pack_kernel(steps, levels, width, level_ref, *refs):
    count = len(refs) - len(steps)
    level = level_ref[0]
    for step, out_ref in zip(steps, refs[count:], strict=True):
        column = pl.multiple_of(partner(level, step, levels) * width, HEAD_DIM)
        for place, ref in enumerate(refs[:count]):
            rows = ref.shape[0]
            out_ref[pl.ds(place * rows, rows), :] = ref[:, pl.ds(column, width)]


def pack(level, arrays, steps, levels, width):
    rows = arrays[0].shape[0] * len(arrays)
    vmem = pl.BlockSpec(memory_space=pltpu.VMEM)
    return pl.pallas_call(
        functools.partial(pack_kernel, steps, levels, width),
        out_shape=[pltpu.VMEM((rows, width), arrays[0].dtype)] * len(steps),
        in_specs=[pl.BlockSpec(memory_space=pltpu.SMEM)] + [vmem] * len(arrays),
        out_specs=[vmem] * len(steps),
    )(level, *arrays)


def attend_kernel(places, rows, heads_here, sides, others, gate_ref, *refs):
    levels = len(places)
    fresh = refs[: sides * levels]
    stale = refs[sides * levels : sides * (levels + others)]
    outs = refs[sides * (levels + others) :]
    nearest = (((1,), (1,)), ((), ()))
    plain = (((1,), (0,)), ((), ()))
    for head in range(heads_here):
        columns = slice(head * HEAD_DIM, (head + 1) * HEAD_DIM)
        query = jnp.concatenate([r[0:rows, columns] for r in fresh[:levels]], axis=0)
        keys = [r[rows : 2 * rows, columns] for r in fresh]
        values = [r[2 * rows : 3 * rows, columns] for r in fresh]
        for r in stale:
            keys += [r[i, 0:rows, columns] for i in range(levels)]
            values += [r[i, rows : 2 * rows, columns] for i in range(levels)]
        key = jnp.concatenate(keys, axis=0)
        value = jnp.concatenate(values, axis=0)
        score = lax.dot_general(
            query, key, nearest, preferred_element_type=jnp.float32
        ) * HEAD_DIM ** (-0.5)
        expo = jnp.exp(score - jnp.max(score, axis=-1, keepdims=True))
        total = jnp.sum(expo, axis=-1, keepdims=True)
        summed = lax.dot_general(
            expo.astype(jnp.bfloat16), value, plain, preferred_element_type=jnp.float32
        )
        gated = ((summed / total) * gate_ref[0:1, columns]).astype(jnp.bfloat16)
        for place, out_ref in zip(places, outs, strict=True):
            out_ref[:, columns] = gated[place * rows : (place + 1) * rows, :]


def join_kernel(steps, levels, width, level_ref, *refs):
    out_ref = refs[-1]
    level = level_ref[0]
    for step, ref in zip(steps, refs[:-1], strict=True):
        column = pl.multiple_of(source(level, step, levels) * width, HEAD_DIM)
        out_ref[:, pl.ds(column, width)] = ref[...]


def body_few(queries, keys_new, values_new, keys_old, values_old, gate_table, step_index):
    groups = lax.axis_size("uly")
    patches = lax.axis_size("patch")
    lane = 2
    levels = groups // lane
    heads_here = HEADS // levels
    width = heads_here * HEAD_DIM
    rows = queries.shape[0]
    level = lax.axis_index("uly").astype(jnp.int32) // lane
    index = level.reshape(1)
    stale_steps = steps = steps_of(levels)
    out_steps = out_steps_of(levels)
    places = [steps.index(step) for step in out_steps]
    vmem = pl.BlockSpec(memory_space=pltpu.VMEM)
    smem = pl.BlockSpec(memory_space=pltpu.SMEM)

    def exchange(pieces, order, way):
        result = [pieces[0]]
        for step, piece in zip(order[1:], pieces[1:], strict=True):
            result.append(shift(piece, "uly", step, lane, levels, way))
        return result

    def swap_all(pieces):
        result = []
        for piece in pieces:
            result.append(swap(piece))
        return result

    stale_out = pack(index, (keys_old, values_old), stale_steps, levels, width)
    stale_here = jnp.stack(exchange(stale_out, stale_steps, partner))
    fresh_out = pack(index, (queries, keys_new, values_new), steps, levels, width)
    gate_here = lax.dynamic_slice(gate_table, (step_index[0], level * width), (1, width))
    stale_here, fresh_out, gate_here = lax.optimization_barrier((stale_here, fresh_out, gate_here))
    stale = []
    for step in reversed(range(1, patches)):
        stale.append(shift(stale_here, "patch", step, 1, patches))
    fresh = exchange(fresh_out, steps, partner)
    stale += swap_all(stale)
    fresh += swap_all(fresh)

    attended = pl.pallas_call(
        functools.partial(attend_kernel, places, rows, heads_here, lane, patches - 1),
        out_shape=[pltpu.VMEM((rows, width), jnp.bfloat16)] * levels,
        in_specs=[vmem] * (1 + len(fresh) + len(stale)),
        out_specs=[vmem] * levels,
        name="attend",
    )(*[in_vmem(x) for x in (gate_here, *fresh, *stale)])
    pieces = exchange(attended, out_steps, source)
    return pl.pallas_call(
        functools.partial(join_kernel, out_steps, levels, width),
        out_shape=jax.ShapeDtypeStruct((rows, levels * width), jnp.bfloat16),
        in_specs=[smem] + [vmem] * levels,
        out_specs=vmem,
        name="join",
    )(index, *[in_vmem(x) for x in pieces])


def solution(mesh):
    direct = 1 < mesh.shape["patch"] <= MAX_DIRECT and mesh.shape["uly"] % 4 == 0
    body = body_few if direct else body_many
    in_specs = (
        P(("patch", "uly"), None),
        P(("patch", "uly"), None),
        P(("patch", "uly"), None),
        P(("patch", "uly"), None),
        P(("patch", "uly"), None),
        P(),
        P(),
    )
    out_specs = P(("patch", "uly"), None)

    return jax.shard_map(body, mesh=mesh, in_specs=in_specs, out_specs=out_specs, check_vma=False)
```

```python
import functools

import jax
import jax.numpy as jnp
from jax import lax
from jax.experimental import pallas as pl
from jax.experimental.pallas import tpu as pltpu
from jax.sharding import PartitionSpec as P


HEADS = 24
HEAD_DIM = 128
MAX_DIRECT = 8


def absorb(carry, query_heads, key_piece, value_piece, masked):
    run_max, run_total, accumulated = carry
    score = jnp.einsum(
        "phd,khd->hpk", query_heads, key_piece, preferred_element_type=jnp.float32
    ) * HEAD_DIM ** (-0.5)
    score = jnp.where(masked[None, None, :], jnp.float32(-1e30), score)
    new_max = jnp.maximum(run_max, jnp.max(score, axis=-1))
    shrink = jnp.exp(run_max - new_max)
    expo = jnp.exp(score - new_max[..., None])
    run_total = run_total * shrink + jnp.sum(expo, axis=-1)
    update = jnp.einsum(
        "hpk,khd->phd", expo.astype(jnp.bfloat16), value_piece, preferred_element_type=jnp.float32
    )
    accumulated = accumulated * jnp.transpose(shrink)[..., None] + update
    return (new_max, run_total, accumulated)


def absorb_blocks(carry, query_heads, key_piece, value_piece, masked):
    count = key_piece.shape[0]
    span = 2048
    if count > span and count % span == 0:
        heads_here = key_piece.shape[1]
        key_blocks = key_piece.reshape(count // span, span, heads_here, HEAD_DIM)
        value_blocks = value_piece.reshape(count // span, span, heads_here, HEAD_DIM)
        mask_blocks = masked.reshape(count // span, span)

        def one_block(state, pieces):
            return (absorb(state, query_heads, pieces[0], pieces[1], pieces[2]), None)

        carry, _ = lax.scan(one_block, carry, (key_blocks, value_blocks, mask_blocks))
        return carry
    return absorb(carry, query_heads, key_piece, value_piece, masked)


def body_many(queries, keys_new, values_new, keys_old, values_old, gate_table, step_index):
    groups = lax.axis_size("uly")
    heads_here = HEADS // groups
    width_here = heads_here * HEAD_DIM
    patch_here = lax.axis_index("patch")
    fresh = (
        lax.all_to_all(queries, "uly", split_axis=1, concat_axis=0, tiled=True),
        lax.all_to_all(keys_new, "uly", split_axis=1, concat_axis=0, tiled=True),
        lax.all_to_all(values_new, "uly", split_axis=1, concat_axis=0, tiled=True),
    )
    query_heads = fresh[0].reshape(-1, heads_here, HEAD_DIM)
    fresh_keys = fresh[1].reshape(-1, heads_here, HEAD_DIM)
    fresh_values = fresh[2].reshape(-1, heads_here, HEAD_DIM)
    patch_rows = query_heads.shape[0]
    score = jnp.einsum(
        "phd,khd->hpk", query_heads, fresh_keys, preferred_element_type=jnp.float32
    ) * HEAD_DIM ** (-0.5)
    run_max = jnp.max(score, axis=-1)
    expo = jnp.exp(score - run_max[..., None])
    run_total = jnp.sum(expo, axis=-1)
    accumulated = jnp.einsum(
        "hpk,khd->phd", expo.astype(jnp.bfloat16), fresh_values, preferred_element_type=jnp.float32
    )
    carry = (run_max, run_total, accumulated)
    stale = (
        lax.all_to_all(keys_old, "uly", split_axis=1, concat_axis=0, tiled=True),
        lax.all_to_all(values_old, "uly", split_axis=1, concat_axis=0, tiled=True),
    )
    stale_keys = stale[0].reshape(-1, heads_here, HEAD_DIM)
    stale_values = stale[1].reshape(-1, heads_here, HEAD_DIM)
    pieces = (
        lax.all_gather(stale_keys, "patch", axis=0, tiled=True),
        lax.all_gather(stale_values, "patch", axis=0, tiled=True),
    )
    count = pieces[0].shape[0]
    masked = jnp.arange(count, dtype=jnp.int32) // patch_rows == patch_here
    carry = absorb_blocks(carry, query_heads, pieces[0], pieces[1], masked)
    run_max, run_total, accumulated = carry
    picker = (jnp.arange(gate_table.shape[0], dtype=jnp.int32) == step_index[0]).astype(jnp.float32)
    gate = jnp.dot(picker, gate_table, precision=lax.Precision.HIGHEST)
    gate_here = lax.dynamic_slice_in_dim(gate, lax.axis_index("uly") * width_here, width_here, 0)
    mixed = (accumulated / jnp.transpose(run_total)[..., None]).reshape(patch_rows, width_here)
    gated = (mixed * gate_here).astype(jnp.bfloat16)
    return lax.all_to_all(gated, "uly", split_axis=0, concat_axis=1, tiled=True)


def steps_of(count):
    return [0] + list(range(max(count // 2, 1), count)) + list(reversed(range(1, count // 2)))


def out_steps_of(count):
    return [0] + list(reversed(range(1, count)))


def partner(here, step, count):
    if count & (count - 1) == 0:
        return here ^ step
    return (here + step) % count


def source(here, step, count):
    if count & (count - 1) == 0:
        return here ^ step
    return (here - step) % count


def shift(array, axis, step, lane, count, way=partner):
    pairs = [(i * lane + j, way(i, step, count) * lane + j) for i in range(count) for j in range(lane)]
    return lax.ppermute(array, axis, pairs)


def swap(array):
    return lax.ppermute(array, "uly", [(i, i ^ 1) for i in range(lax.axis_size("uly"))])


def in_vmem(array):
    return pltpu.with_memory_space_constraint(array, pltpu.VMEM)


def pack_kernel(steps, levels, width, level_ref, *refs):
    count = len(refs) - len(steps)
    level = level_ref[0]
    for step, out_ref in zip(steps, refs[count:], strict=True):
        column = pl.multiple_of(partner(level, step, levels) * width, HEAD_DIM)
        for place, ref in enumerate(refs[:count]):
            rows = ref.shape[0]
            out_ref[pl.ds(place * rows, rows), :] = ref[:, pl.ds(column, width)]


def pack(level, arrays, steps, levels, width):
    rows = arrays[0].shape[0] * len(arrays)
    vmem = pl.BlockSpec(memory_space=pltpu.VMEM)
    return pl.pallas_call(
        functools.partial(pack_kernel, steps, levels, width),
        out_shape=[pltpu.VMEM((rows, width), arrays[0].dtype)] * len(steps),
        in_specs=[pl.BlockSpec(memory_space=pltpu.SMEM)] + [vmem] * len(arrays),
        out_specs=[vmem] * len(steps),
    )(level, *arrays)


def attend_kernel(places, rows, heads_here, sides, others, gate_ref, *refs):
    levels = len(places)
    fresh = refs[: sides * levels]
    stale = refs[sides * levels : sides * (levels + others)]
    outs = refs[sides * (levels + others) :]
    nearest = (((1,), (1,)), ((), ()))
    plain = (((1,), (0,)), ((), ()))

    def scores(head):
        columns = slice(head * HEAD_DIM, (head + 1) * HEAD_DIM)
        query = jnp.concatenate([r[0:rows, columns] for r in fresh[:levels]], axis=0)
        keys = [r[rows : 2 * rows, columns] for r in fresh]
        for r in stale:
            keys += [r[i, 0:rows, columns] for i in range(levels)]
        key = jnp.concatenate(keys, axis=0)
        return lax.dot_general(query, key, nearest, preferred_element_type=jnp.float32)

    def weights(raw):
        score = raw * HEAD_DIM ** (-0.5)
        expo = jnp.exp(score - jnp.max(score, axis=-1, keepdims=True))
        return expo.astype(jnp.bfloat16), jnp.sum(expo, axis=-1, keepdims=True)

    def finish(head, weight, total):
        columns = slice(head * HEAD_DIM, (head + 1) * HEAD_DIM)
        values = [r[2 * rows : 3 * rows, columns] for r in fresh]
        for r in stale:
            values += [r[i, rows : 2 * rows, columns] for i in range(levels)]
        value = jnp.concatenate(values, axis=0)
        summed = lax.dot_general(weight, value, plain, preferred_element_type=jnp.float32)
        gated = ((summed / total) * gate_ref[0:1, columns]).astype(jnp.bfloat16)
        for place, out_ref in zip(places, outs, strict=True):
            out_ref[:, columns] = gated[place * rows : (place + 1) * rows, :]

    raw = [scores(head) for head in range(heads_here)]
    soft = [weights(one) for one in raw]
    for head, (weight, total) in enumerate(soft):
        finish(head, weight, total)


def join_kernel(steps, levels, width, level_ref, *refs):
    out_ref = refs[-1]
    level = level_ref[0]
    for step, ref in zip(steps, refs[:-1], strict=True):
        column = pl.multiple_of(source(level, step, levels) * width, HEAD_DIM)
        out_ref[:, pl.ds(column, width)] = ref[...]


def body_few(queries, keys_new, values_new, keys_old, values_old, gate_table, step_index):
    groups = lax.axis_size("uly")
    patches = lax.axis_size("patch")
    lane = 2
    levels = groups // lane
    heads_here = HEADS // levels
    width = heads_here * HEAD_DIM
    rows = queries.shape[0]
    level = lax.axis_index("uly").astype(jnp.int32) // lane
    index = level.reshape(1)
    stale_steps = steps = steps_of(levels)
    out_steps = out_steps_of(levels)
    places = [steps.index(step) for step in out_steps]
    vmem = pl.BlockSpec(memory_space=pltpu.VMEM)
    smem = pl.BlockSpec(memory_space=pltpu.SMEM)

    def exchange(pieces, order, way):
        result = [pieces[0]]
        for step, piece in zip(order[1:], pieces[1:], strict=True):
            result.append(shift(piece, "uly", step, lane, levels, way))
        return result

    def swap_all(pieces):
        result = []
        for piece in pieces:
            result.append(swap(piece))
        return result

    stale_out = pack(index, (keys_old, values_old), stale_steps, levels, width)
    stale_here = jnp.stack(exchange(stale_out, stale_steps, partner))
    fresh_out = pack(index, (queries, keys_new, values_new), steps, levels, width)
    gate_here = lax.dynamic_slice(gate_table, (step_index[0], level * width), (1, width))
    stale_here, fresh_out, gate_here = lax.optimization_barrier((stale_here, fresh_out, gate_here))
    stale = []
    for step in reversed(range(1, patches)):
        stale.append(shift(stale_here, "patch", step, 1, patches))
    fresh = exchange(fresh_out, steps, partner)
    stale += swap_all(stale)
    fresh += swap_all(fresh)

    attended = pl.pallas_call(
        functools.partial(attend_kernel, places, rows, heads_here, lane, patches - 1),
        out_shape=[pltpu.VMEM((rows, width), jnp.bfloat16)] * levels,
        in_specs=[vmem] * (1 + len(fresh) + len(stale)),
        out_specs=[vmem] * levels,
        name="attend",
    )(*[in_vmem(x) for x in (gate_here, *fresh, *stale)])
    pieces = exchange(attended, out_steps, source)
    return pl.pallas_call(
        functools.partial(join_kernel, out_steps, levels, width),
        out_shape=jax.ShapeDtypeStruct((rows, levels * width), jnp.bfloat16),
        in_specs=[smem] + [vmem] * levels,
        out_specs=vmem,
        name="join",
    )(index, *[in_vmem(x) for x in pieces])


def solution(mesh):
    direct = 1 < mesh.shape["patch"] <= MAX_DIRECT and mesh.shape["uly"] % 4 == 0
    body = body_few if direct else body_many
    in_specs = (
        P(("patch", "uly"), None),
        P(("patch", "uly"), None),
        P(("patch", "uly"), None),
        P(("patch", "uly"), None),
        P(("patch", "uly"), None),
        P(),
        P(),
    )
    out_specs = P(("patch", "uly"), None)

    return jax.shard_map(body, mesh=mesh, in_specs=in_specs, out_specs=out_specs, check_vma=False)
```
